32 devices in a mesh: row: 4 (over y, x), col: 8 (over z, core).
Axes of the slice: x: 2, y: 2, z: 4, core: 2. Of those that a mesh axis runs over, the one named last changes fastest.
Arguments:
- correlation: float32 [8192, 8192], P('row', 'col'), may hold values from -8 to 32, as said below
- coeff: float32 [8192, 2, 8192], P('row', None, 'col'), may hold values from -6 to 6
Outputs:
- factored: float32 [8192, 8192], P('row', 'col')
- coeff_out: float32 [8192, 2, 8192], P('row', None, 'col')
The draws below stay inside these ranges and needn't reach their ends.
Inputs may be any that keep to these rules, and one draw needn't show every extreme that they name: correlation is symmetric and positive definite, with smallest eigenvalue above 0.1.
All inputs are finite; a program needn't handle non-finite values.
Results may differ from the reference program's by a relative error of at most 0.0001.
Values sent between devices are 32-bit elements; how exact they have to be, the bound alone decides.
A program may use at most 128 MiB of HBM per device.

```python
import math
import jax
import jax.numpy as jnp
from jax import lax

NB = 8192
PB = 256
PANELS = 2
NPW = 8192


def draw_correlation(key, part):
    first = jax.random.fold_in(key, 0)
    second = jax.random.fold_in(key, 1)
    fourth = jax.random.fold_in(key, 3)
    noise = jax.random.normal(first, (NB, NB), jnp.float32)
    matrix = (noise + noise.T) * (0.35 / math.sqrt(NB))
    diagonal = jax.random.uniform(second, (NB,), jnp.float32, 1.5, 3.0)
    spread_rank = 2 * PB
    factor = jax.random.normal(fourth, (NB, spread_rank), jnp.float32) * math.sqrt(3.0 / spread_rank)
    gram = jnp.dot(factor, factor.T, precision=lax.Precision.HIGHEST, preferred_element_type=jnp.float32)
    gram = 0.5 * (gram + gram.T)
    matrix = matrix + gram + jnp.diag(diagonal)
    return matrix


def steps_of(rng, shape, cuts, least, largest):
    level = 1.0
    for axis_at, parts in cuts:
        steps = jax.random.uniform(jax.random.fold_in(jax.random.fold_in(rng, 6), axis_at), (parts,), jnp.float32, least / len(cuts), largest / len(cuts))
        level = level * jnp.repeat(jnp.exp(steps), shape[axis_at] // parts).reshape((-1,) + (1,) * (len(shape) - 1 - axis_at))
    return level


def gaussian(own_key, shape, scale, reach, cuts=(), kind=jnp.bfloat16):
    gain = steps_of(own_key, shape, cuts, -0.22, 0.18) if cuts else 1.0
    drawn = jax.random.normal(own_key, shape, jnp.float32) * scale * gain
    return jnp.minimum(jnp.maximum(drawn, -reach), reach).astype(kind)


def setup_inputs(seed: int = 0) -> dict:
    key_list = jax.random.split(jax.random.key(seed), 3)
    correlation = draw_correlation(jax.random.fold_in(key_list[2], 71), 0)
    coeff = gaussian(key_list[1], (NB, 2, NPW), 1.0, 6.0, ((0, 4), (2, 8)), jnp.float32)
    return dict(correlation=correlation, coeff=coeff)


def reference(correlation, coeff):
    width = PANELS * PB
    work = correlation
    bands = jnp.arange(NB)
    pieces = []
    for panel in range(PANELS):
        start = panel * PB
        chol = jnp.linalg.cholesky(work[start:start + PB, start:start + PB])
        solved = lax.linalg.triangular_solve(chol, work[:, start:start + PB].T, left_side=True, lower=True).T
        keep = bands[:, None] - start >= jnp.arange(PB)[None, :]
        lpanel = jnp.where(keep, solved, 0.0)
        work = work - jnp.dot(lpanel.astype(jnp.float32), lpanel.T.astype(jnp.float32), precision=lax.Precision.HIGHEST, preferred_element_type=jnp.float32)
        pieces.append(lpanel)
    lfactor = jnp.concatenate(pieces, axis=1)
    padded = jnp.pad(lfactor, ((0, 0), (0, NB - width)))
    factored = jnp.where(bands[None, :] < width, padded, jnp.where(bands[:, None] < width, 0.0, work))
    flat = coeff.reshape(NB, -1)
    top = lax.linalg.triangular_solve(lfactor[:width], flat[:width], left_side=True, lower=True)
    rest = flat - jnp.dot(lfactor.astype(jnp.float32), top.astype(jnp.float32), precision=lax.Precision.HIGHEST, preferred_element_type=jnp.float32)
    merged = jnp.concatenate([top, rest[width:]], axis=0)
    return (factored, merged.reshape(coeff.shape))
```

```python
import jax
import jax.numpy as jnp
from jax import lax
from jax.experimental import pallas as pl
from jax.experimental.pallas import tpu as pltpu
from jax.sharding import PartitionSpec as P

PB = 256
PANELS = 2
BLOCK = 128
EXACT = lax.Precision.HIGHEST


def spread(value, axes):
    first = True
    for axis in axes:
        first = jnp.logical_and(first, lax.axis_index(axis) == 0)
    kept = jnp.where(first, value, 0).astype(value.dtype)
    return lax.psum(kept, axes)


def tree(value, axis, count, descending):
    strides = []
    stride = 1
    while stride < count:
        strides.append(stride)
        stride *= 2
    if descending:
        strides.reverse()
    index = lax.axis_index(axis)
    holders = [0]
    for stride in strides:
        pairs = [(h, h + stride) for h in holders if h + stride < count]
        received = lax.ppermute(value, axis, pairs)
        target = False
        for _, dest in pairs:
            target = jnp.logical_or(target, index == dest)
        value = jnp.where(target, received, value)
        holders = holders + [dest for _, dest in pairs]
    return value


def dot(a, b, dims, precision=EXACT):
    return lax.dot_general(
        a, b, (dims, ((), ())), precision=precision, preferred_element_type=jnp.float32
    )


def block_inverse(block):
    size = block.shape[0]
    rows = lax.broadcasted_iota(jnp.int32, (size, size), 0)
    cols = lax.broadcasted_iota(jnp.int32, (size, size), 1)
    left = [block[i : i + 8] for i in range(0, size, 8)]
    eye = jnp.where(rows == cols, 1.0, 0.0).astype(jnp.float32)
    right = [eye[i : i + 8] for i in range(0, size, 8)]
    sub = lax.broadcasted_iota(jnp.int32, (8, 1), 0)
    for j in range(size):
        at, k = divmod(j, 8)
        lrow = left[at][k : k + 1]
        rrow = right[at][k : k + 1]
        recip = 1.0 / lrow[:, j : j + 1]
        lscaled = lrow * recip
        rscaled = rrow * recip
        for t in range(at, size // 8):
            factor = left[t][:, j : j + 1]
            if t == at:
                factor = jnp.where(sub > k, factor, 0.0)
            left[t] = left[t] - factor * lscaled
            right[t] = right[t] - factor * rscaled
    reduced = jnp.concatenate(left, axis=0)
    inverse = jnp.concatenate(right, axis=0)
    pivots = jnp.sum(jnp.where(rows == cols, reduced, 0.0), axis=1, keepdims=True)
    return inverse / jnp.sqrt(pivots)


def inverse_kernel(a_ref, out_ref, s_ref, l_ref):
    width = a_ref.shape[0]
    s_ref[...] = a_ref[...]
    out_ref[...] = jnp.zeros_like(out_ref)
    l_ref[...] = jnp.zeros_like(l_ref)

    def step(b, carry):
        start = pl.multiple_of(b * BLOCK, BLOCK)
        here = pl.ds(start, BLOCK)
        inverse = block_inverse(s_ref[here, here])
        sums = dot(l_ref[here, :], out_ref[...], ((1,), (0,)))
        out_ref[here, :] = -dot(inverse, sums, ((1,), (0,)))
        out_ref[here, here] = inverse
        panel = dot(s_ref[:, here], inverse, ((1,), (1,)))
        rows = lax.broadcasted_iota(jnp.int32, panel.shape, 0)
        panel = jnp.where(rows >= start + BLOCK, panel, 0.0)
        l_ref[:, here] = panel
        s_ref[...] = s_ref[...] - dot(panel, panel, ((1,), (1,)))
        return carry

    lax.fori_loop(0, width // BLOCK, step, 0)


def factor_inverse(block):
    width = block.shape[0]
    return pl.pallas_call(
        inverse_kernel,
        out_shape=jax.ShapeDtypeStruct(block.shape, jnp.float32),
        in_specs=[pl.BlockSpec(memory_space=pltpu.VMEM)],
        out_specs=pl.BlockSpec(memory_space=pltpu.VMEM),
        scratch_shapes=[pltpu.VMEM(block.shape, jnp.float32)] * 2,
        cost_estimate=pl.CostEstimate(
            flops=100_000 * width * width, bytes_accessed=8 * width * width, transcendentals=0
        ),
    )(block)


def shards(sizes, correlation, coeff):
    rows_local, cols_local = correlation.shape
    width = PANELS * PB
    rows_global = lax.axis_index("row") * rows_local + jnp.arange(rows_local)
    cols_global = lax.axis_index("col") * cols_local + jnp.arange(cols_local)
    bands = jnp.arange(width)

    lead = spread(correlation[:width, :width], ("row", "col"))
    flat = coeff.reshape(rows_local, -1)
    half = flat.shape[1] // 2
    raw_top = jnp.concatenate(
        [
            tree(flat[:width, :half], "row", sizes["row"], False),
            tree(flat[:width, half:], "row", sizes["row"], True),
        ],
        axis=1,
    )
    mid = cols_local // 2
    raw_cols = jnp.concatenate(
        [
            tree(correlation[:width, :mid], "row", sizes["row"], False),
            tree(correlation[:width, mid:], "row", sizes["row"], True),
        ],
        axis=1,
    )
    raw_rows = spread(correlation[:, :width], ("col",))

    inverse = factor_inverse(lead)
    top = dot(inverse, raw_top, ((1,), (0,)))
    factor_cols = dot(inverse, raw_cols, ((1,), (0,)))
    factor_cols = jnp.where(cols_global[None, :] >= bands[:, None], factor_cols, 0.0)
    lfactor = dot(raw_rows, inverse, ((1,), (1,)))
    lfactor = jnp.where(rows_global[:, None] >= bands[None, :], lfactor, 0.0)

    work = correlation - dot(lfactor, factor_cols, ((1,), (0,)), lax.Precision.HIGH)
    padded = jnp.pad(lfactor, ((0, 0), (0, cols_local - width)))
    factored = jnp.where(
        cols_global[None, :] < width, padded, jnp.where(rows_global[:, None] < width, 0.0, work)
    )
    rest = flat - dot(lfactor, top, ((1,), (0,)), lax.Precision.HIGH)
    placed = jnp.pad(top, ((0, rows_local - width), (0, 0)))
    merged = jnp.where(rows_global[:, None] < width, placed, rest)
    return (factored, merged.reshape(coeff.shape))


def solution(mesh):
    sizes = dict(mesh.shape)
    return jax.shard_map(
        lambda correlation, coeff: shards(sizes, correlation, coeff),
        mesh=mesh,
        in_specs=(P("row", "col"), P("row", None, "col")),
        out_specs=(P("row", "col"), P("row", None, "col")),
        check_vma=False,
    )
```
